256 devices in a mesh: grp: 8 (over x, core), ctx: 32 (over z, y).
Axes of the slice: x: 4, y: 4, z: 8, core: 2. Of those that a mesh axis runs over, the one named last changes fastest.
Arguments:
- queries: bfloat16 [32768, 4096], P(('grp', 'ctx')), parts along dimension 0, may hold values from -8 to 8
- key_states: bfloat16 [32768, 512], P(('grp', 'ctx')), parts along dimension 0, may hold values from -8 to 8
- value_states: bfloat16 [32768, 512], P(('grp', 'ctx')), parts along dimension 0, may hold values from -6 to 6
- grads_out: bfloat16 [32768, 4096], P(('grp', 'ctx')), parts along dimension 0, may hold values from -6 to 6
- doc_lengths: int32 [64], P('grp'), parts along dimension 0, may hold values from 1 to 1024, as said below
- block_plan: int32 [512], P('grp'), parts along dimension 0, may hold values from 0 to 63, as said below
- needed: int32 [256, 8], P('grp'), parts along dimension 0, may hold values from 0 to 63, as said below
Outputs:
- outputs: bfloat16 [32768, 4096], P(('grp', 'ctx')), parts along dimension 0
- query_grads: bfloat16 [32768, 4096], P(('grp', 'ctx')), parts along dimension 0
- key_grads: bfloat16 [32768, 512], P(('grp', 'ctx')), parts along dimension 0
- value_grads: bfloat16 [32768, 512], P(('grp', 'ctx')), parts along dimension 0
The draws below stay inside these ranges and needn't reach their ends.
There are 8 independent parts, one for each index of `grp`. The reference program is written for one: setup_inputs(seed, part) draws one part's arguments, and reference() takes and returns one part's arrays. A program takes and returns all parts, laid end to end along the dimension named above; each array names one. Nothing has to cross between parts.
Inputs may be any that keep to these rules, and one draw needn't show every extreme that they name: `doc_lengths`: the lengths sum to 4096 and one of them is exactly 1024. `block_plan`: each block position appears once. `needed`: each row lists 8 different stored block numbers, no two of which have the same value of block number // 2.
All inputs are finite; a program needn't handle non-finite values.
Results may differ from the reference program's by a relative error of at most 0.013.
Values may be sent and summed in bfloat16 or wider, within the bound.
No kernel may reach another device: no remote copies, remote signals or barrier semaphores. Data moves between devices by JAX's collectives and lax.ppermute only.
A program may use at most 128 MiB of HBM per device.

```python
import math
import jax
import jax.numpy as jnp
from jax import lax

HEADS = 32
KV_HEADS = 4
HEAD_DIM = 128
BLK = 64
NDOC = 8
TOK_DEV = 128
NBLK = 64
TOKENS = 4096
NEED = 8
N_CTX = 32


def plan_parts(key):
    base = jax.random.fold_in(key, 7001)
    big_key, weight_key, plan_key, rank_key = jax.random.split(base, 4)
    doc_slots = jnp.arange(NDOC, dtype=jnp.int32)
    big_doc = jax.random.randint(big_key, (), 0, NDOC, dtype=jnp.int32)
    weights = jnp.where(doc_slots == big_doc, 0, jax.random.randint(weight_key, (NDOC,), 2, 5, dtype=jnp.int32))
    remaining = TOKENS - TOKENS // 4
    shares = remaining * weights // jnp.sum(weights)
    shares = shares + jnp.where(doc_slots == (big_doc + 1) % NDOC, remaining - jnp.sum(shares), 0)
    lengths = jnp.where(doc_slots == big_doc, TOKENS // 4, shares).astype(jnp.int32)
    plan = jax.random.permutation(plan_key, NBLK).astype(jnp.int32)
    return (lengths, plan, rank_key)


def draw_queries(key, part):
    normal_key = jax.random.fold_in(jax.random.fold_in(key, 11), 0)
    sampled = jnp.clip(jax.random.normal(normal_key, (TOKENS, HEADS * HEAD_DIM), jnp.float32), -6.0, 6.0)
    return sampled.astype(jnp.bfloat16)


def draw_key_states(key, part):
    sampled = jnp.clip(jax.random.normal(jax.random.fold_in(key, 13), (TOKENS, KV_HEADS * HEAD_DIM), jnp.float32), -6.0, 6.0)
    return sampled.astype(jnp.bfloat16)


def draw_doc_lengths(key, part):
    lengths, plan, rank_key = plan_parts(key)
    return lengths


def draw_block_plan(key, part):
    lengths, plan, rank_key = plan_parts(key)
    return plan


def draw_needed(key, part):
    lengths, plan, rank_key = plan_parts(key)
    ends = jnp.cumsum(lengths).astype(jnp.int32)

    def doc_of(points):
        return jnp.sum((ends[None, :] <= points[:, None]).astype(jnp.int32), axis=1)
    first_doc = doc_of(plan * BLK)
    last_doc = doc_of(plan * BLK + BLK - 1)
    owners = NBLK // 2
    owner_ids = jnp.arange(owners, dtype=jnp.int32)
    query_blocks = jnp.stack([2 * owner_ids, 2 * owner_ids + 1], axis=1)
    query_plan = jnp.take(plan, query_blocks)
    query_first = jnp.take(first_doc, query_blocks)
    useful = (plan[None, None, :] < query_plan[:, :, None]) & (last_doc[None, None, :] == query_first[:, :, None])
    useful = jnp.any(useful, axis=1)
    ranks = jax.vmap(lambda row_key: jax.random.permutation(row_key, NBLK))(jax.random.split(rank_key, owners))
    score = useful.astype(jnp.int32) * NBLK + ranks.astype(jnp.int32)
    paired = score.reshape(owners, owners, 2)
    second = (paired[:, :, 1] > paired[:, :, 0]).astype(jnp.int32)
    owner_score = jnp.max(paired, axis=2)
    owner_block = 2 * owner_ids[None, :] + second
    order = jnp.argsort(-owner_score, axis=1, stable=True)[:, :NEED]
    return jnp.take_along_axis(owner_block, order, axis=1).astype(jnp.int32)


def steps_of(rng, shape, shards, low, top_value):
    gain = 1.0
    for position, shards_of in shards:
        steps = jax.random.uniform(jax.random.fold_in(jax.random.fold_in(rng, 6), position), (shards_of,), jnp.float32, low / len(shards), top_value / len(shards))
        gain = gain * jnp.repeat(jnp.exp(steps), shape[position] // shards_of).reshape((-1,) + (1,) * (len(shape) - 1 - position))
    return gain


def noise(key, extent, scale, bound, cuts=(), held_as=jnp.bfloat16):
    values = scale * jax.random.normal(key, extent, jnp.float32)
    if cuts:
        values = values * steps_of(key, extent, cuts, -0.22, 0.18)
    return jnp.clip(values, -bound, bound).astype(held_as)


def setup_inputs(seed: int = 0, part: int = 0) -> dict:
    key_list = jax.random.split(jax.random.key(seed), 8)
    part_splits = jax.random.split(jax.random.fold_in(key_list[7], part), 8)
    queries = draw_queries(jax.random.fold_in(jax.random.fold_in(key_list[7], part), 71), part)
    key_states = draw_key_states(jax.random.fold_in(jax.random.fold_in(key_list[7], part), 71), part)
    value_states = noise(part_splits[2], (TOKENS, KV_HEADS * HEAD_DIM), 1.0, 6.0, ((0, 32),))
    grads_out = noise(part_splits[3], (TOKENS, HEADS * HEAD_DIM), 1.0, 6.0, ((0, 32),))
    doc_lengths = draw_doc_lengths(jax.random.fold_in(jax.random.fold_in(key_list[7], part), 71), part)
    block_plan = draw_block_plan(jax.random.fold_in(jax.random.fold_in(key_list[7], part), 71), part)
    needed = draw_needed(jax.random.fold_in(jax.random.fold_in(key_list[7], part), 71), part)
    return dict(queries=queries, key_states=key_states, value_states=value_states, grads_out=grads_out, doc_lengths=doc_lengths, block_plan=block_plan, needed=needed)


masked_score = -1e+30

def token_labels(block_plan, doc_ends):
    stored = jnp.arange(TOKENS, dtype=jnp.int32)
    stored_block = stored // BLK
    placed = jnp.take(block_plan, stored_block).astype(jnp.int32) * BLK + stored % BLK
    documents = lax.optimization_barrier(jnp.sum((doc_ends[None, :] <= placed[:, None]).astype(jnp.int32), axis=1))
    return (stored_block, placed, documents)

def reference(queries, key_states, value_states, grads_out, doc_lengths, block_plan, needed):
    score_scale = 1.0 / math.sqrt(HEAD_DIM)
    group_heads = HEADS // KV_HEADS
    doc_ends = jnp.cumsum(doc_lengths).astype(jnp.int32)
    key_block, key_place, key_doc = token_labels(block_plan, doc_ends)
    keys_grouped = key_states.astype(jnp.float32).reshape(TOKENS, KV_HEADS, HEAD_DIM)
    values_grouped = value_states.astype(jnp.float32).reshape(TOKENS, KV_HEADS, HEAD_DIM)

    def per_rank(carried, inputs):
        key_sum, value_sum = carried
        rank_queries, rank_grads, wanted, own_rank = inputs
        first_row = own_rank * TOK_DEV
        query_block = lax.dynamic_slice_in_dim(key_block, first_row, TOK_DEV)
        query_place = lax.dynamic_slice_in_dim(key_place, first_row, TOK_DEV)
        query_doc = lax.dynamic_slice_in_dim(key_doc, first_row, TOK_DEV)
        listed = jnp.any(wanted[:, None] == key_block[None, :], axis=0)
        allowed = listed[None, :] | (query_block[:, None] == key_block[None, :])
        visible_pairs = allowed & (query_doc[:, None] == key_doc[None, :]) & (key_place[None, :] <= query_place[:, None])
        grouped = rank_queries.astype(jnp.float32).reshape(TOK_DEV, KV_HEADS, group_heads, HEAD_DIM)
        scores = jnp.einsum('qhgd,khd->hgqk', grouped, keys_grouped) * score_scale
        scores = jnp.where(visible_pairs, scores, masked_score)
        highest = lax.optimization_barrier(jnp.max(scores, axis=-1))
        totals = lax.optimization_barrier(jnp.sum(jnp.where(visible_pairs, jnp.exp(scores - highest[..., None]), 0.0), axis=-1))
        log_total = highest + jnp.log(totals)
        soft_weights = jnp.where(visible_pairs, jnp.exp(scores - log_total[..., None]), 0.0)
        probs_low = lax.optimization_barrier(soft_weights.astype(jnp.bfloat16)).astype(jnp.float32)
        attended = jnp.einsum('hgqk,khd->qhgd', soft_weights, values_grouped)
        outputs = attended.reshape(TOK_DEV, HEADS * HEAD_DIM).astype(jnp.bfloat16)
        gradient_rows = rank_grads.astype(jnp.float32).reshape(TOK_DEV, KV_HEADS, group_heads, HEAD_DIM)
        products = gradient_rows * outputs.astype(jnp.float32).reshape(TOK_DEV, KV_HEADS, group_heads, HEAD_DIM)
        row_delta = jnp.transpose(lax.optimization_barrier(jnp.sum(products, axis=-1)), (1, 2, 0))
        prob_grads = jnp.einsum('qhgd,khd->hgqk', gradient_rows, values_grouped)
        score_grads = (soft_weights * (prob_grads - row_delta[..., None])).astype(jnp.bfloat16)
        score_grads = lax.optimization_barrier(score_grads).astype(jnp.float32)
        query_part = jnp.einsum('hgqk,khd->qhgd', score_grads, keys_grouped) * score_scale
        query_grads = query_part.reshape(TOK_DEV, HEADS * HEAD_DIM).astype(jnp.bfloat16)
        key_part = jnp.einsum('hgqk,qhgd->khd', score_grads, grouped) * score_scale
        value_part = jnp.einsum('hgqk,qhgd->khd', probs_low, gradient_rows)
        key_low = lax.optimization_barrier(key_part.reshape(TOKENS, -1).astype(jnp.bfloat16))
        value_low = lax.optimization_barrier(value_part.reshape(TOKENS, -1).astype(jnp.bfloat16))
        key_sum = key_sum + key_low.astype(jnp.float32)
        value_sum = value_sum + value_low.astype(jnp.float32)
        return ((key_sum, value_sum), (outputs, query_grads))
    empty_sum = jnp.zeros((TOKENS, KV_HEADS * HEAD_DIM), jnp.float32)
    inputs = (queries.reshape(N_CTX, TOK_DEV, HEADS * HEAD_DIM), grads_out.reshape(N_CTX, TOK_DEV, HEADS * HEAD_DIM), needed, jnp.arange(N_CTX, dtype=jnp.int32))
    sums, stacked = lax.scan(per_rank, (empty_sum, empty_sum), inputs)
    outputs = stacked[0].reshape(TOKENS, HEADS * HEAD_DIM)
    query_grads = stacked[1].reshape(TOKENS, HEADS * HEAD_DIM)
    return (outputs, query_grads, sums[0].astype(jnp.bfloat16), sums[1].astype(jnp.bfloat16))
```

```python
import math

import jax
import jax.numpy as jnp
from jax import lax
from jax.experimental import pallas as pl
from jax.experimental.pallas import tpu as pltpu
from jax.sharding import Mesh
from jax.sharding import PartitionSpec as P

HEADS = 32
KV_HEADS = 4
HEAD_DIM = 128
GROUP = HEADS // KV_HEADS
BLK = 64
NEED = 8
NDOC = 8
TOK = 128
ZN = 8
YN = 4
KVW = KV_HEADS * HEAD_DIM
KEYS = TOK + NEED * BLK
PAIR = 2 * TOK
SCALE = 1.0 / math.sqrt(HEAD_DIM)
LOG2E = math.log2(math.e)
HIDDEN = -1e30

BUNDLES = ((0,), (1, -1), (2, -2), (3, -3), (4,))

VM = pl.BlockSpec(memory_space=pltpu.VMEM)
SM = pl.BlockSpec(memory_space=pltpu.SMEM)


def half(ref, part):
    return ref.at[pl.ds(pl.multiple_of(part * BLK, BLK), BLK), :]


def wants_second(needed, rank, owner):
    found = jnp.int32(0)
    for j in range(NEED):
        found = jnp.where(needed[rank, j] == 2 * owner + 1, 1, found)
    return found


def pack(needed, shards, offsets):
    count = len(offsets)

    def body(needed, *refs):
        ins, outs = refs[: len(shards)], refs[len(shards) :]
        z, y = lax.axis_index("z"), lax.axis_index("y")
        for m in (1, 2, 3):
            rank = z * YN + lax.rem(y + m, YN)
            for i, k in enumerate(offsets):
                owner = lax.rem(z + k + ZN, ZN) * YN + y
                part = wants_second(needed, rank, owner)
                dst = outs[m - 1].at[pl.ds(i * BLK, BLK), :]
                if k == 4:

                    @pl.when(part == 0)
                    def _():
                        dst[...] = ins[0][...]

                    @pl.when(part == 1)
                    def _():
                        dst[...] = ins[1][...]
                else:
                    dst[...] = half(ins[i], part)[...]

    return pl.pallas_call(
        body,
        out_shape=[jax.ShapeDtypeStruct((count * BLK, 2 * KVW), jnp.bfloat16)] * 3,
        in_specs=[SM] + [VM] * len(shards),
        out_specs=[VM] * 3,
        name="pack",
    )(needed, *shards)


def shift(array, axis, size, by):
    return lax.ppermute(array, axis, [(i, (i + by) % size) for i in range(size)])


def to_mates(arrays, sign):
    return [shift(a, "y", YN, sign * m) for m, a in zip((1, 2, 3), arrays)]


def join(key_states, value_states):
    def body(k, v, kv):
        kv[:, :KVW] = k[...]
        kv[:, KVW:] = v[...]

    return pl.pallas_call(
        body,
        out_shape=jax.ShapeDtypeStruct((TOK, 2 * KVW), jnp.bfloat16),
        in_specs=[VM, VM],
        out_specs=VM,
        name="join",
    )(key_states, value_states)


def gather(kv, needed):
    shards = {0: kv}
    received = {0: to_mates(pack(needed, [kv], (0,)), 1)}
    low, high = kv, kv
    for step in (1, 2, 3):
        low, high = shift(low, "z", ZN, 1), shift(high, "z", ZN, -1)
        shards[-step], shards[step] = low, high
        offsets = (step, -step)
        received[step] = to_mates(pack(needed, [high, low], offsets), 1)
    far = [shift(low[:BLK], "z", ZN, 1), shift(high[BLK:], "z", ZN, -1)]
    received[4] = to_mates(pack(needed, far, (4,)), 1)
    return shards, far, received


def attend_body(needed, plan, lengths, q_ref, do_ref, *refs):
    n_in = 7 + 2 + 15
    ins, refs = refs[:n_in], refs[n_in:]
    o_ref, dq_ref, refs = refs[0], refs[1], refs[2:]
    n_out = 1 + 7 + 15
    outs, refs = refs[:n_out], refs[n_out:]
    kv, grad, bias, table, qs, dos, pt, dst = refs
    g = pl.program_id(0)
    z, y = lax.axis_index("z"), lax.axis_index("y")
    me = z * YN + y
    shards = dict(zip((0, 1, -1, 2, -2, 3, -3), ins[:7]))
    far = ins[7:9]
    received = {b: ins[9 + 3 * b : 12 + 3 * b] for b in range(5)}
    own_out = outs[0]
    col_out = dict(zip((1, -1, 2, -2, 3, -3, 4), outs[1:8]))
    mate_out = {b: outs[8 + 3 * b : 11 + 3 * b] for b in range(5)}

    def slot_rows(j):
        return pl.ds(pl.multiple_of(TOK + j * BLK, BLK), BLK)

    @pl.when(g == 0)
    def _():
        for i in range(YN * ZN):
            table[i] = -1
        for j in range(NEED):
            owner = needed[me, j] // 2
            distance = lax.rem(owner // YN - z + ZN, ZN)
            mate = lax.rem(y - lax.rem(owner, YN) + YN, YN)
            table[mate * ZN + distance] = j

        kv[:TOK, :] = shards[0][...]
        for b, offsets in enumerate(BUNDLES):
            for i, k in enumerate(offsets):
                j = table[k % ZN]
                part = needed[me, jnp.maximum(j, 0)] % 2
                if k == 4:

                    @pl.when((j >= 0) & (part == 0))
                    def _():
                        kv[slot_rows(j), :] = far[0][...]

                    @pl.when((j >= 0) & (part == 1))
                    def _():
                        kv[slot_rows(j), :] = far[1][...]
                else:

                    @pl.when(j >= 0)
                    def _():
                        kv[slot_rows(j), :] = half(shards[k], part)[...]

                for m in (1, 2, 3):
                    jm = table[m * ZN + k % ZN]

                    @pl.when(jm >= 0)
                    def _():
                        kv[slot_rows(jm), :] = received[b][m - 1][pl.ds(i * BLK, BLK), :]

        ends, total = [], jnp.int32(0)
        for d in range(NDOC):
            total = total + lengths[d]
            ends.append(total)

        def docs(place):
            found = jnp.zeros_like(place)
            for end in ends:
                found = found + (place >= end).astype(jnp.int32)
            return found

        lane = lax.broadcasted_iota(jnp.int32, (BLK, TOK), 1)
        first = lane < BLK
        q_place = jnp.where(first, plan[2 * me] * BLK, plan[2 * me + 1] * BLK) + lane % BLK
        q_doc = docs(q_place)
        row = lax.broadcasted_iota(jnp.int32, (BLK, TOK), 0)

        def block_bias(block, allowed):
            k_place = plan[block] * BLK + row
            seen = (docs(k_place) == q_doc) & (k_place <= q_place) & allowed
            return jnp.where(seen, 0.0, HIDDEN)

        for half_block in (0, 1):
            block = 2 * me + half_block
            listed = jnp.int32(0)
            for j in range(NEED):
                listed = jnp.where(needed[me, j] == block, 1, listed)
            same = (lane // BLK) == half_block
            bias[half_block * BLK : (half_block + 1) * BLK, :] = block_bias(
                block, same | ((row * 0 + listed) == 1)
            )
        for j in range(NEED):
            block = needed[me, j]
            other = jnp.where(block // 2 == me, 0, 1)
            bias[TOK + j * BLK : TOK + (j + 1) * BLK, :] = block_bias(block, (row * 0 + other) == 1)

    for h in range(GROUP):
        qs[h * TOK : (h + 1) * TOK, :] = q_ref[:, h * HEAD_DIM : (h + 1) * HEAD_DIM]
        dos[h * TOK : (h + 1) * TOK, :] = do_ref[:, h * HEAD_DIM : (h + 1) * HEAD_DIM]

    k_cols = pl.ds(pl.multiple_of(g * HEAD_DIM, HEAD_DIM), HEAD_DIM)
    v_cols = pl.ds(pl.multiple_of(KVW + g * HEAD_DIM, HEAD_DIM), HEAD_DIM)
    keys, values = kv[:, k_cols], kv[:, v_cols]
    keys_t, values_t = keys.T, values.T
    wide_bias = jnp.concatenate([bias[...]] * 2, axis=1)

    def nt(a, b):
        return lax.dot_general(a, b, (((1,), (1,)), ((), ())), preferred_element_type=jnp.float32)

    def nn(a, b):
        return jnp.dot(a, b, preferred_element_type=jnp.float32)

    for pair in range(GROUP // 2):
        rows = slice(pair * PAIR, (pair + 1) * PAIR)
        scores = nt(keys, qs[rows, :]) * (SCALE * LOG2E) + wide_bias
        highest = jnp.max(scores, axis=0, keepdims=True)
        weights = jnp.exp2(scores - highest)
        weights = weights * (1.0 / jnp.sum(weights, axis=0, keepdims=True))
        low = weights.astype(jnp.bfloat16)
        pt[:, rows] = low
        out = nn(values_t, low).T
        prob_grads = nt(values, dos[rows, :])
        delta = jnp.sum(weights * prob_grads, axis=0, keepdims=True)
        score_grads = (weights * (prob_grads - delta)).astype(jnp.bfloat16)
        dst[:, rows] = score_grads
        dq = (nn(keys_t, score_grads) * SCALE).T
        for i in range(2):
            cols = slice((2 * pair + i) * HEAD_DIM, (2 * pair + i + 1) * HEAD_DIM)
            o_ref[:, cols] = out[i * TOK : (i + 1) * TOK, :].astype(jnp.bfloat16)
            dq_ref[:, cols] = dq[i * TOK : (i + 1) * TOK, :].astype(jnp.bfloat16)
    grad[:, k_cols] = (nn(dst[...], qs[...]) * SCALE).astype(jnp.bfloat16)
    grad[:, v_cols] = nn(pt[...], dos[...]).astype(jnp.bfloat16)

    @pl.when(g == KV_HEADS - 1)
    def _():
        own_out[...] = grad[:TOK, :]
        blank = jnp.zeros((BLK, 2 * KVW), jnp.bfloat16)
        for b, offsets in enumerate(BUNDLES):
            for i, k in enumerate(offsets):
                if k != 0:
                    col_out[k][:BLK, :] = blank
                    col_out[k][BLK:, :] = blank
                    j = table[k % ZN]
                    part = needed[me, jnp.maximum(j, 0)] % 2

                    @pl.when(j >= 0)
                    def _():
                        half(col_out[k], part)[...] = grad[slot_rows(j), :]

                for m in (1, 2, 3):
                    jm = table[m * ZN + k % ZN]
                    target = mate_out[b][m - 1].at[pl.ds(i * BLK, BLK), :]

                    @pl.when(jm >= 0)
                    def _():
                        target[...] = grad[slot_rows(jm), :]

                    @pl.when(jm < 0)
                    def _():
                        target[...] = blank


def attend(queries, grads_out, lengths, plan, needed, shards, far, received):
    block = pl.BlockSpec((TOK, GROUP * HEAD_DIM), lambda g: (0, g))
    ins = [shards[k] for k in (0, 1, -1, 2, -2, 3, -3)] + far
    for b in range(5):
        ins += received[b]
    bf = jnp.bfloat16
    wide = jax.ShapeDtypeStruct((TOK, HEADS * HEAD_DIM), bf)
    shard = jax.ShapeDtypeStruct((TOK, 2 * KVW), bf)
    outs = [wide, wide] + [shard] * 8
    for offsets in BUNDLES:
        outs += [jax.ShapeDtypeStruct((len(offsets) * BLK, 2 * KVW), bf)] * 3
    got = pl.pallas_call(
        attend_body,
        grid=(KV_HEADS,),
        out_shape=outs,
        in_specs=[SM] * 3 + [block] * 2 + [VM] * len(ins),
        out_specs=[block] * 2 + [VM] * (len(outs) - 2),
        scratch_shapes=[
            pltpu.VMEM((KEYS, 2 * KVW), bf),
            pltpu.VMEM((KEYS, 2 * KVW), bf),
            pltpu.VMEM((KEYS, TOK), jnp.float32),
            pltpu.SMEM((YN * ZN,), jnp.int32),
            pltpu.VMEM((GROUP * TOK, HEAD_DIM), bf),
            pltpu.VMEM((GROUP * TOK, HEAD_DIM), bf),
            pltpu.VMEM((KEYS, GROUP * TOK), bf),
            pltpu.VMEM((KEYS, GROUP * TOK), bf),
        ],
        compiler_params=pltpu.CompilerParams(vmem_limit_bytes=48 << 20),
        name="attend",
    )(needed, plan, lengths, queries, grads_out, *ins)
    outputs, query_grads, own = got[:3]
    column = dict(zip((1, -1, 2, -2, 3, -3, 4), got[3:10]))
    mates = {b: got[10 + 3 * b : 13 + 3 * b] for b in range(5)}
    return outputs, query_grads, own, column, mates


def combine(needed, column, arrived, ring, offsets):
    last = offsets == (0,)
    n_col, n_ring = len(column), len(ring)

    def body(needed, *refs):
        cols, refs = refs[:n_col], refs[n_col:]
        mates, refs = refs[:3], refs[3:]
        rings, refs = refs[:n_ring], refs[n_ring:]
        outs, acc = refs[:-1], refs[-1]
        z, y = lax.axis_index("z"), lax.axis_index("y")
        for i, k in enumerate(offsets):
            acc[...] = cols[i][...].astype(jnp.float32)
            owner = lax.rem(z + k + ZN, ZN) * YN + y
            for m in (1, 2, 3):
                rank = z * YN + lax.rem(y + m, YN)
                part = wants_second(needed, rank, owner)
                spot = half(acc, part)
                spot[...] += mates[m - 1][i * BLK : (i + 1) * BLK, :].astype(jnp.float32)
            if last:
                for r in rings:
                    acc[...] += r[...].astype(jnp.float32)
                outs[0][...] = acc[:, :KVW].astype(jnp.bfloat16)
                outs[1][...] = acc[:, KVW:].astype(jnp.bfloat16)
            elif k == 4:
                outs[0][...] = acc[:BLK, :].astype(jnp.bfloat16)
                outs[1][...] = acc[BLK:, :].astype(jnp.bfloat16)
            else:
                if abs(k) == 3:
                    where = slice(0, BLK) if k > 0 else slice(BLK, TOK)
                    acc[where, :] += rings[i][...].astype(jnp.float32)
                else:
                    acc[...] += rings[i][...].astype(jnp.float32)
                outs[i][...] = acc[...].astype(jnp.bfloat16)

    if last:
        shapes = [(TOK, KVW)] * 2
    elif offsets == (4,):
        shapes = [(BLK, 2 * KVW)] * 2
    else:
        shapes = [(TOK, 2 * KVW)] * 2
    return pl.pallas_call(
        body,
        out_shape=[jax.ShapeDtypeStruct(s, jnp.bfloat16) for s in shapes],
        in_specs=[SM] + [VM] * (n_col + 3 + n_ring),
        out_specs=[VM] * 2,
        scratch_shapes=[pltpu.VMEM((TOK, 2 * KVW), jnp.float32)],
        name="combine",
    )(needed, *column, *arrived, *ring)


def scatter(own, column, mates, needed):
    ring = []
    arrived = {b: to_mates(mates[b], -1) for b in (4, 3, 2, 1, 0)}
    for b in (4, 3, 2, 1):
        offsets = BUNDLES[b]
        up, down = combine(needed, [column[k] for k in offsets], arrived[b], ring, offsets)
        ring = [shift(up, "z", ZN, 1), shift(down, "z", ZN, -1)]
    return combine(needed, [own], arrived[0], ring, (0,))


def on_device(queries, key_states, value_states, grads_out, lengths, plan, needed):
    kv = join(key_states, value_states)
    shards, far, received = gather(kv, needed)
    outputs, query_grads, own, column, mates = attend(
        queries, grads_out, lengths, plan, needed, shards, far, received
    )
    key_grads, value_grads = scatter(own, column, mates, needed)
    return outputs, query_grads, key_grads, value_grads


def solution(mesh):
    torus = Mesh(mesh.devices.reshape(mesh.shape["grp"], ZN, YN), ("grp", "z", "y"))
    rows = P(("grp", "z", "y"), None)
    return jax.shard_map(
        on_device,
        mesh=torus,
        in_specs=(rows, rows, rows, rows, P("grp"), P("grp"), P("grp", None)),
        out_specs=(rows, rows, rows, rows),
        check_vma=False,
    )
```

```python
import math

import jax
import jax.numpy as jnp
from jax import lax
from jax.experimental import pallas as pl
from jax.experimental.pallas import tpu as pltpu
from jax.sharding import Mesh
from jax.sharding import PartitionSpec as P

HEADS = 32
KV_HEADS = 4
HEAD_DIM = 128
GROUP = HEADS // KV_HEADS
BLK = 64
NEED = 8
NDOC = 8
TOK = 128
ZN = 8
YN = 4
KVW = KV_HEADS * HEAD_DIM
KEYS = TOK + NEED * BLK
PAIR = 2 * TOK
SCALE = 1.0 / math.sqrt(HEAD_DIM)
LOG2E = math.log2(math.e)
HIDDEN = -1e30

FETCH = ((0, 1, -1, 2, -2), (3, -3, 4))
GIVE = ((3, -3), (2, -2, 4), (1, -1), (0,))
COLUMN = (0, 1, -1, 2, -2, 3, -3, 4)

VM = pl.BlockSpec(memory_space=pltpu.VMEM)
ANY = pl.BlockSpec(memory_space=pl.ANY)
FAR = pl.BlockSpec(memory_space=pltpu.HBM)
SM = pl.BlockSpec(memory_space=pltpu.SMEM)


def half(ref, part):
    return ref.at[pl.ds(pl.multiple_of(part * BLK, BLK), BLK), :]


def like(rows, cols=2 * KVW):
    return jax.ShapeDtypeStruct((rows, cols), jnp.bfloat16)


def listed(needed, rank, block):
    found = jnp.int32(0)
    for j in range(NEED):
        found = jnp.where(needed[j, rank] == block, 1, found)
    return found


def each_listed(needed, offsets, do):
    z, y = lax.axis_index("z"), lax.axis_index("y")
    for i, k in enumerate(offsets):
        owner = lax.rem(z + k + ZN, ZN) * YN + y
        for m in (1, 2, 3):
            rank = z * YN + lax.rem(y + m, YN)
            first, second = (listed(needed, rank, 2 * owner + p) for p in (0, 1))

            @pl.when(first + second > 0)
            def _(i=i, m=m, second=second):
                do(m, i, second)


def pack(needed, shards, offsets):
    count = len(offsets)

    def body(needed, *refs):
        ins, outs, sems = refs[:count], refs[count:-1], refs[-1]

        def copy(m, i, part):
            dst = outs[m - 1].at[pl.ds(i * BLK, BLK), :]
            return pltpu.make_async_copy(half(ins[i], part), dst, sems.at[i, m - 1])

        each_listed(needed, offsets, lambda *at: copy(*at).start())
        each_listed(needed, offsets, lambda *at: copy(*at).wait())

    return pl.pallas_call(
        body,
        out_shape=[like(count * BLK)] * 3,
        in_specs=[SM] + [ANY] * count,
        out_specs=[VM] * 3,
        scratch_shapes=[pltpu.SemaphoreType.DMA((count, 3))],
        name="pack",
    )(needed, *shards)


def shift(array, axis, size, by):
    return lax.ppermute(array, axis, [(i, (i + by) % size) for i in range(size)])


def to_mates(arrays, sign):
    return [shift(a, "y", YN, sign * m) for m, a in zip((1, 2, 3), arrays)]


def join(key_states, value_states):
    def body(k, v, kv):
        kv[:, :KVW] = k[...]
        kv[:, KVW:] = v[...]

    return pl.pallas_call(
        body,
        out_shape=like(TOK),
        in_specs=[VM, VM],
        out_specs=VM,
        name="join",
    )(key_states, value_states)


def gather(kv, needed):
    shards = {0: kv}
    shards[1], shards[-1] = shift(kv, "z", ZN, -1), shift(kv, "z", ZN, 1)
    shards[2], shards[-2] = shift(shards[1], "z", ZN, -1), shift(shards[-1], "z", ZN, 1)

    def packed(b):
        return pack(needed, [shards[k] for k in FETCH[b]], FETCH[b])

    mine = packed(0)
    first = to_mates(mine, 1)
    up, down, far, mine = lax.optimization_barrier((shards[2], shards[-2], kv, mine))
    shards[3], shards[-3] = shift(up, "z", ZN, -1), shift(down, "z", ZN, 1)
    shards[4] = shift(far, "z", ZN, 4)
    return shards, [first, to_mates(packed(1), 1)]


def attend_body(needed, plan, lengths, q_ref, do_ref, *refs):
    shards, refs = dict(zip(COLUMN, refs[:ZN])), refs[ZN:]
    received, refs = [refs[3 * b : 3 * b + 3] for b in range(len(FETCH))], refs[3 * len(FETCH) :]
    o_ref, dq_ref, grad_out, refs = refs[0], refs[1], refs[2], refs[3:]
    mate_out, refs = [refs[3 * b : 3 * b + 3] for b in range(len(GIVE))], refs[3 * len(GIVE) :]
    kv, grad, bias, table, qs, dos, pt, dst, sems = refs
    g = pl.program_id(0)
    z, y = lax.axis_index("z"), lax.axis_index("y")
    me = z * YN + y

    def slot_rows(j):
        return pl.ds(pl.multiple_of(TOK + j * BLK, BLK), BLK)

    def each_source(bundles, do):
        for b, offsets in enumerate(bundles):
            for i, k in enumerate(offsets):
                for m in range(YN):
                    j = table[m * ZN + k % ZN]

                    @pl.when(j >= 0)
                    def _(j=j, b=b, i=i, m=m, k=k):
                        do(j, b, i, m, k)

    @pl.when(g == 0)
    def _():
        own_copy = pltpu.make_async_copy(shards[0], kv.at[pl.ds(0, TOK), :], sems.at[NEED])
        own_copy.start()
        for i in range(YN * ZN):
            table[i] = -1
        for j in range(NEED):
            owner = needed[j, me] // 2
            distance = lax.rem(owner // YN - z + ZN, ZN)
            mate = lax.rem(y - lax.rem(owner, YN) + YN, YN)
            table[mate * ZN + distance] = j

        def fetch(j, b, i, m, k):
            if m == 0:
                src = half(shards[k], needed[j, me] % 2)
            else:
                src = received[b][m - 1].at[pl.ds(i * BLK, BLK), :]
            pltpu.make_async_copy(src, kv.at[slot_rows(j), :], sems.at[j]).start()

        each_source(FETCH, fetch)
        ends, total = [], jnp.int32(0)
        for d in range(NDOC):
            total = total + lengths[d]
            ends.append(total)

        def docs(place):
            found = jnp.zeros_like(place)
            for end in ends:
                found = found + (place >= end).astype(jnp.int32)
            return found

        lane = lax.broadcasted_iota(jnp.int32, (BLK, TOK), 1)
        first = lane < BLK
        q_place = jnp.where(first, plan[2 * me] * BLK, plan[2 * me + 1] * BLK) + lane % BLK
        q_doc = docs(q_place)
        row = lax.broadcasted_iota(jnp.int32, (BLK, TOK), 0)

        def block_bias(block, allowed):
            k_place = plan[block] * BLK + row
            seen = (docs(k_place) == q_doc) & (k_place <= q_place) & allowed
            return jnp.where(seen, 0.0, HIDDEN)

        for half_block in (0, 1):
            block = 2 * me + half_block
            also = listed(needed, me, block)
            same = (lane // BLK) == half_block
            bias[half_block * BLK : (half_block + 1) * BLK, :] = block_bias(
                block, same | ((row * 0 + also) == 1)
            )
        for j in range(NEED):
            block = needed[j, me]
            other = jnp.where(block // 2 == me, 0, 1)
            bias[TOK + j * BLK : TOK + (j + 1) * BLK, :] = block_bias(block, (row * 0 + other) == 1)
        own_copy.wait()
        for j in range(NEED):
            slot = kv.at[pl.ds(TOK + j * BLK, BLK), :]
            pltpu.make_async_copy(half(shards[0], 0), slot, sems.at[j]).wait()

    for h in range(GROUP):
        qs[h * TOK : (h + 1) * TOK, :] = q_ref[:, h * HEAD_DIM : (h + 1) * HEAD_DIM]
        dos[h * TOK : (h + 1) * TOK, :] = do_ref[:, h * HEAD_DIM : (h + 1) * HEAD_DIM]

    k_cols = pl.ds(pl.multiple_of(g * HEAD_DIM, HEAD_DIM), HEAD_DIM)
    v_cols = pl.ds(pl.multiple_of(KVW + g * HEAD_DIM, HEAD_DIM), HEAD_DIM)
    keys, values = kv[:, k_cols], kv[:, v_cols]
    wide_bias = jnp.concatenate([bias[...]] * 2, axis=1)

    def nt(a, b):
        return lax.dot_general(a, b, (((1,), (1,)), ((), ())), preferred_element_type=jnp.float32)

    def tn(a, b):
        return lax.dot_general(a, b, (((0,), (0,)), ((), ())), preferred_element_type=jnp.float32)

    def nn(a, b):
        return jnp.dot(a, b, preferred_element_type=jnp.float32)

    for pair in range(GROUP // 2):
        rows = slice(pair * PAIR, (pair + 1) * PAIR)
        scores = nt(keys, qs[rows, :]) * (SCALE * LOG2E) + wide_bias
        highest = jnp.max(scores, axis=0, keepdims=True)
        weights = jnp.exp2(scores - highest)
        weights = weights * (1.0 / jnp.sum(weights, axis=0, keepdims=True))
        low = weights.astype(jnp.bfloat16)
        pt[:, rows] = low
        prob_grads = nt(values, dos[rows, :])
        delta = jnp.sum(weights * prob_grads, axis=0, keepdims=True)
        score_grads = (weights * (prob_grads - delta)).astype(jnp.bfloat16)
        dst[:, rows] = score_grads
    out = tn(pt[...], values)
    dq = tn(dst[...], keys) * SCALE
    for h in range(GROUP):
        cols, rows = slice(h * HEAD_DIM, (h + 1) * HEAD_DIM), slice(h * TOK, (h + 1) * TOK)
        o_ref[:, cols] = out[rows, :].astype(jnp.bfloat16)
        dq_ref[:, cols] = dq[rows, :].astype(jnp.bfloat16)
    grad[:, k_cols] = (nn(dst[...], qs[...]) * SCALE).astype(jnp.bfloat16)
    grad[:, v_cols] = nn(pt[...], dos[...]).astype(jnp.bfloat16)

    @pl.when(g == KV_HEADS - 1)
    def _():
        whole = pltpu.make_async_copy(grad, grad_out, sems.at[NEED])
        whole.start()

        def send(j, b, i, m, k):
            if m > 0:
                target = mate_out[b][m - 1].at[pl.ds(i * BLK, BLK), :]
                pltpu.make_async_copy(grad.at[slot_rows(j), :], target, sems.at[j]).start()

        def sent(j, b, i, m, k):
            if m > 0:
                target = mate_out[b][m - 1].at[pl.ds(i * BLK, BLK), :]
                pltpu.make_async_copy(grad.at[slot_rows(j), :], target, sems.at[j]).wait()

        each_source(GIVE, send)
        each_source(GIVE, sent)
        whole.wait()


def attend(queries, grads_out, lengths, plan, needed, shards, received):
    block = pl.BlockSpec((TOK, GROUP * HEAD_DIM), lambda g: (0, g))
    ins = [shards[k] for k in COLUMN]
    for arrays in received:
        ins += arrays
    bf = jnp.bfloat16
    outs = [like(TOK, HEADS * HEAD_DIM)] * 2 + [like(KEYS)]
    for offsets in GIVE:
        outs += [like(len(offsets) * BLK)] * 3
    got = pl.pallas_call(
        attend_body,
        grid=(KV_HEADS,),
        out_shape=outs,
        in_specs=[SM] * 3 + [block] * 2 + [ANY] * len(ins),
        out_specs=[block] * 2 + [ANY] * (len(outs) - 2),
        scratch_shapes=[
            pltpu.VMEM((KEYS, 2 * KVW), bf),
            pltpu.VMEM((KEYS, 2 * KVW), bf),
            pltpu.VMEM((KEYS, TOK), jnp.float32),
            pltpu.SMEM((YN * ZN,), jnp.int32),
            pltpu.VMEM((GROUP * TOK, HEAD_DIM), bf),
            pltpu.VMEM((GROUP * TOK, HEAD_DIM), bf),
            pltpu.VMEM((KEYS, GROUP * TOK), bf),
            pltpu.VMEM((KEYS, GROUP * TOK), bf),
            pltpu.SemaphoreType.DMA((NEED + 1,)),
        ],
        compiler_params=pltpu.CompilerParams(vmem_limit_bytes=56 << 20),
        name="attend",
    )(needed, plan, lengths, queries, grads_out, *ins)
    return got[0], got[1], got[2], [got[3 + 3 * b : 6 + 3 * b] for b in range(len(GIVE))]


def combine(needed, grad, arrived, extra, offsets):
    n = len(offsets)
    home = offsets == (0,)

    def body(needed, grad, *refs):
        mates, refs = refs[:3], refs[3:]
        more, refs = refs[: len(extra)], refs[len(extra) :]
        outs, (acc, own, theirs, along, sems) = refs[:-5], refs[-5:]
        z, y = lax.axis_index("z"), lax.axis_index("y")
        me = z * YN + y

        def from_mate(m, i, part):
            src = mates[m - 1].at[pl.ds(i * BLK, BLK), :]
            return pltpu.make_async_copy(src, theirs.at[i, m - 1], sems.at[i, m])

        def own_slots(do):
            for i, k in enumerate(offsets):
                owner = lax.rem(z + k + ZN, ZN) * YN + y
                for j in range(NEED):

                    @pl.when(needed[j, me] // 2 == owner)
                    def _(i=i, j=j):
                        rows = pl.ds(TOK + j * BLK, BLK)
                        do(pltpu.make_async_copy(grad.at[rows, :], own.at[i], sems.at[i, 0]), i, j)

        ring = [
            pltpu.make_async_copy(r, along.at[e], sems.at[n, e]) for e, r in enumerate(more)
        ]
        for c in ring:
            c.start()
        each_listed(needed, offsets, lambda *at: from_mate(*at).start())
        if home:
            mine = pltpu.make_async_copy(grad.at[pl.ds(0, TOK), :], own, sems.at[0, 0])
            mine.start()
            mine.wait()
            acc[0] = own[...].astype(jnp.float32)
        else:
            own_slots(lambda c, i, j: c.start())
            if not ring:
                acc[...] = jnp.zeros_like(acc)
        for e, c in enumerate(ring):
            c.wait()
            if home:
                acc[0] += along[e].astype(jnp.float32)
            else:
                acc[e] = along[e].astype(jnp.float32)
        if n > len(ring) and ring:
            acc[n - 1] = jnp.zeros((TOK, 2 * KVW), jnp.float32)

        def add_mate(m, i, part):
            from_mate(m, i, part).wait()
            half(acc.at[i], part)[...] += theirs[i, m - 1].astype(jnp.float32)

        def add_own(c, i, j):
            c.wait()
            half(acc.at[i], needed[j, me] % 2)[...] += own[i].astype(jnp.float32)

        each_listed(needed, offsets, add_mate)
        if home:
            outs[0][...] = acc[0, :, :KVW].astype(jnp.bfloat16)
            outs[1][...] = acc[0, :, KVW:].astype(jnp.bfloat16)
        else:
            own_slots(add_own)
            for i in range(n):
                outs[i][...] = acc[i].astype(jnp.bfloat16)

    shapes = [like(TOK, KVW)] * 2 if home else [like(TOK)] * n
    return pl.pallas_call(
        body,
        out_shape=shapes,
        in_specs=[SM, FAR] + [ANY] * (3 + len(extra)),
        out_specs=[VM] * len(shapes),
        scratch_shapes=[
            pltpu.VMEM((n, TOK, 2 * KVW), jnp.float32),
            pltpu.VMEM((TOK, 2 * KVW) if home else (n, BLK, 2 * KVW), jnp.bfloat16),
            pltpu.VMEM((n, 3, BLK, 2 * KVW), jnp.bfloat16),
            pltpu.VMEM((max(len(extra), 1), TOK, 2 * KVW), jnp.bfloat16),
            pltpu.SemaphoreType.DMA((n + 1, YN)),
        ],
        compiler_params=pltpu.CompilerParams(vmem_limit_bytes=16 << 20),
        name="combine",
    )(needed, grad, *arrived, *extra)


def scatter(grad, mates, needed):
    def hop(arrays):
        return [shift(arrays[0], "z", ZN, 1), shift(arrays[1], "z", ZN, -1)]

    third = to_mates(mates[0], -1)
    second = to_mates(mates[1], -1)
    ring = list(combine(needed, grad, third, [], GIVE[0]))
    first, last, ring[0] = lax.optimization_barrier((mates[2], mates[3], ring[0]))
    first = to_mates(first, -1)
    ring = hop(ring)
    up, down, far = combine(needed, grad, second, ring, GIVE[1])
    last, up = lax.optimization_barrier((last, up))
    far = shift(far, "z", ZN, 4)
    ring = hop([up, down])
    last = to_mates(last, -1)
    ring = hop(combine(needed, grad, first, ring, GIVE[2]))
    return combine(needed, grad, last, ring + [far], GIVE[3])


def on_device(queries, key_states, value_states, grads_out, lengths, plan, needed):
    needed = needed.T
    shards, received = gather(join(key_states, value_states), needed)
    outputs, query_grads, grad, mates = attend(
        queries, grads_out, lengths, plan, needed, shards, received
    )
    key_grads, value_grads = scatter(grad, mates, needed)
    return outputs, query_grads, key_grads, value_grads


def solution(mesh):
    torus = Mesh(mesh.devices.reshape(mesh.shape["grp"], ZN, YN), ("grp", "z", "y"))
    rows = P(("grp", "z", "y"), None)
    return jax.shard_map(
        on_device,
        mesh=torus,
        in_specs=(rows, rows, rows, rows, P("grp"), P("grp"), P("grp", None)),
        out_specs=(rows, rows, rows, rows),
        check_vma=False,
    )
```

```python
import math

import jax
import jax.numpy as jnp
from jax import lax
from jax.experimental import pallas as pl
from jax.experimental.pallas import tpu as pltpu
from jax.sharding import Mesh
from jax.sharding import PartitionSpec as P

HEADS = 32
KV_HEADS = 4
HEAD_DIM = 128
GROUP = HEADS // KV_HEADS
BLK = 64
NEED = 8
NDOC = 8
TOK = 128
ZN = 8
YN = 4
KVW = KV_HEADS * HEAD_DIM
KEYS = TOK + NEED * BLK
PAIR = 2 * TOK
SCALE = 1.0 / math.sqrt(HEAD_DIM)
LOG2E = math.log2(math.e)
HIDDEN = -1e30

FETCH = ((0,), (1, -1, 2, -2), (3, -3, 4))
GIVE = ((3, -3), (2, -2, 4), (1, -1), (0,))
COLUMN = (0, 1, -1, 2, -2, 3, -3, 4)

VM = pl.BlockSpec(memory_space=pltpu.VMEM)
ANY = pl.BlockSpec(memory_space=pl.ANY)
SM = pl.BlockSpec(memory_space=pltpu.SMEM)


def half(ref, part):
    return ref.at[pl.ds(pl.multiple_of(part * BLK, BLK), BLK), :]


def like(rows, cols=2 * KVW):
    return jax.ShapeDtypeStruct((rows, cols), jnp.bfloat16)


def listed(needed, rank, block):
    found = jnp.int32(0)
    for j in range(NEED):
        found = jnp.where(needed[j, rank] == block, 1, found)
    return found


def each_listed(needed, offsets, do):
    z, y = lax.axis_index("z"), lax.axis_index("y")
    for i, k in enumerate(offsets):
        owner = lax.rem(z + k + ZN, ZN) * YN + y
        for m in (1, 2, 3):
            rank = z * YN + lax.rem(y + m, YN)
            first, second = (listed(needed, rank, 2 * owner + p) for p in (0, 1))

            @pl.when(first + second > 0)
            def _(i=i, m=m, second=second):
                do(m, i, second)


def pack(needed, shards, offsets):
    count = len(offsets)

    def body(needed, *refs):
        ins, outs, sems = refs[:count], refs[count:-1], refs[-1]

        def copy(m, i, part):
            dst = outs[m - 1].at[pl.ds(i * BLK, BLK), :]
            return pltpu.make_async_copy(half(ins[i], part), dst, sems.at[i, m - 1])

        each_listed(needed, offsets, lambda *at: copy(*at).start())
        each_listed(needed, offsets, lambda *at: copy(*at).wait())

    return pl.pallas_call(
        body,
        out_shape=[like(count * BLK)] * 3,
        in_specs=[SM] + [ANY] * count,
        out_specs=[VM] * 3,
        scratch_shapes=[pltpu.SemaphoreType.DMA((count, 3))],
        name="pack",
    )(needed, *shards)


def shift(array, axis, size, by):
    return lax.ppermute(array, axis, [(i, (i + by) % size) for i in range(size)])


def to_mates(arrays, sign):
    return [shift(a, "y", YN, sign * m) for m, a in zip((1, 2, 3), arrays)]


def join(needed, key_states, value_states):
    def body(needed, k, v, kv, *outs):
        kv[:, :KVW] = k[...]
        kv[:, KVW:] = v[...]

        def copy(m, i, part):
            outs[m - 1][:, :KVW] = half(k, part)[...]
            outs[m - 1][:, KVW:] = half(v, part)[...]

        each_listed(needed, (0,), copy)

    got = pl.pallas_call(
        body,
        out_shape=[like(TOK)] + [like(BLK)] * 3,
        in_specs=[SM, VM, VM],
        out_specs=[VM] * 4,
        name="join",
    )(needed, key_states, value_states)
    return got[0], got[1:]


def gather(kv, mine, needed):
    shards = {0: kv}
    shards[1], shards[-1] = shift(kv, "z", ZN, -1), shift(kv, "z", ZN, 1)
    shards[2], shards[-2] = shift(shards[1], "z", ZN, -1), shift(shards[-1], "z", ZN, 1)
    zeroth = to_mates(mine, 1)

    def packed(b):
        return pack(needed, [shards[k] for k in FETCH[b]], FETCH[b])

    shards[2], zeroth = lax.optimization_barrier((shards[2], zeroth))
    mine = packed(1)
    first = to_mates(mine, 1)
    up, down, mine = lax.optimization_barrier((shards[2], shards[-2], mine))
    shards[3], shards[-3] = shift(up, "z", ZN, -1), shift(down, "z", ZN, 1)
    far, shards[3] = lax.optimization_barrier((kv, shards[3]))
    shards[4] = shift(far, "z", ZN, 4)
    return shards, [zeroth, first, to_mates(packed(2), 1)]


def attend_body(needed, plan, lengths, q_ref, do_ref, *refs):
    shards, refs = dict(zip(COLUMN, refs[:ZN])), refs[ZN:]
    received, refs = [refs[3 * b : 3 * b + 3] for b in range(len(FETCH))], refs[3 * len(FETCH) :]
    o_ref, dq_ref, grad_out, refs = refs[0], refs[1], refs[2], refs[3:]
    mate_out, refs = [refs[3 * b : 3 * b + 3] for b in range(len(GIVE))], refs[3 * len(GIVE) :]
    kv, grad, bias, table, qs, dos, pt, dst, sems = refs
    g = pl.program_id(0)
    z, y = lax.axis_index("z"), lax.axis_index("y")
    me = z * YN + y

    def slot_rows(j):
        return pl.ds(pl.multiple_of(TOK + j * BLK, BLK), BLK)

    def each_source(bundles, do):
        for b, offsets in enumerate(bundles):
            for i, k in enumerate(offsets):
                for m in range(YN):
                    j = table[m * ZN + k % ZN]

                    @pl.when(j >= 0)
                    def _(j=j, b=b, i=i, m=m, k=k):
                        do(j, b, i, m, k)

    @pl.when(g == 0)
    def _():
        own_copy = pltpu.make_async_copy(shards[0], kv.at[pl.ds(0, TOK), :], sems.at[NEED])
        own_copy.start()
        for i in range(YN * ZN):
            table[i] = -1
        for j in range(NEED):
            owner = needed[j, me] // 2
            distance = lax.rem(owner // YN - z + ZN, ZN)
            mate = lax.rem(y - lax.rem(owner, YN) + YN, YN)
            table[mate * ZN + distance] = j

        def fetch(j, b, i, m, k):
            if m == 0:
                src = half(shards[k], needed[j, me] % 2)
            else:
                src = received[b][m - 1].at[pl.ds(i * BLK, BLK), :]
            pltpu.make_async_copy(src, kv.at[slot_rows(j), :], sems.at[j]).start()

        each_source(FETCH, fetch)
        ends, total = [], jnp.int32(0)
        for d in range(NDOC):
            total = total + lengths[d]
            ends.append(total)

        def docs(place):
            found = jnp.zeros_like(place)
            for end in ends:
                found = found + (place >= end).astype(jnp.int32)
            return found

        lane = lax.broadcasted_iota(jnp.int32, (BLK, TOK), 1)
        first = lane < BLK
        q_place = jnp.where(first, plan[2 * me] * BLK, plan[2 * me + 1] * BLK) + lane % BLK
        q_doc = docs(q_place)
        row = lax.broadcasted_iota(jnp.int32, (BLK, TOK), 0)

        def block_bias(block, allowed):
            k_place = plan[block] * BLK + row
            seen = (docs(k_place) == q_doc) & (k_place <= q_place) & allowed
            return jnp.where(seen, 0.0, HIDDEN)

        for half_block in (0, 1):
            block = 2 * me + half_block
            also = listed(needed, me, block)
            same = (lane // BLK) == half_block
            bias[half_block * BLK : (half_block + 1) * BLK, :] = block_bias(
                block, same | ((row * 0 + also) == 1)
            )
        for j in range(NEED):
            block = needed[j, me]
            other = jnp.where(block // 2 == me, 0, 1)
            bias[TOK + j * BLK : TOK + (j + 1) * BLK, :] = block_bias(block, (row * 0 + other) == 1)
        own_copy.wait()
        for j in range(NEED):
            slot = kv.at[pl.ds(TOK + j * BLK, BLK), :]
            pltpu.make_async_copy(half(shards[0], 0), slot, sems.at[j]).wait()

    for h in range(GROUP):
        qs[h * TOK : (h + 1) * TOK, :] = q_ref[:, h * HEAD_DIM : (h + 1) * HEAD_DIM]
        dos[h * TOK : (h + 1) * TOK, :] = do_ref[:, h * HEAD_DIM : (h + 1) * HEAD_DIM]

    k_cols = pl.ds(pl.multiple_of(g * HEAD_DIM, HEAD_DIM), HEAD_DIM)
    v_cols = pl.ds(pl.multiple_of(KVW + g * HEAD_DIM, HEAD_DIM), HEAD_DIM)
    keys, values = kv[:, k_cols], kv[:, v_cols]
    wide_bias = jnp.concatenate([bias[...]] * 2, axis=1)

    def nt(a, b):
        return lax.dot_general(a, b, (((1,), (1,)), ((), ())), preferred_element_type=jnp.float32)

    def tn(a, b):
        return lax.dot_general(a, b, (((0,), (0,)), ((), ())), preferred_element_type=jnp.float32)

    def nn(a, b):
        return jnp.dot(a, b, preferred_element_type=jnp.float32)

    for pair in range(GROUP // 2):
        rows = slice(pair * PAIR, (pair + 1) * PAIR)
        scores = nt(keys, qs[rows, :]) * (SCALE * LOG2E) + wide_bias
        highest = jnp.max(scores, axis=0, keepdims=True)
        weights = jnp.exp2(scores - highest)
        weights = weights * (1.0 / jnp.sum(weights, axis=0, keepdims=True))
        low = weights.astype(jnp.bfloat16)
        pt[:, rows] = low
        prob_grads = nt(values, dos[rows, :])
        delta = jnp.sum(weights * prob_grads, axis=0, keepdims=True)
        score_grads = (weights * (prob_grads - delta)).astype(jnp.bfloat16)
        dst[:, rows] = score_grads
    out = tn(pt[...], values)
    dq = tn(dst[...], keys) * SCALE
    for h in range(GROUP):
        cols, rows = slice(h * HEAD_DIM, (h + 1) * HEAD_DIM), slice(h * TOK, (h + 1) * TOK)
        o_ref[:, cols] = out[rows, :].astype(jnp.bfloat16)
        dq_ref[:, cols] = dq[rows, :].astype(jnp.bfloat16)
    grad[:, k_cols] = (nn(dst[...], qs[...]) * SCALE).astype(jnp.bfloat16)
    grad[:, v_cols] = nn(pt[...], dos[...]).astype(jnp.bfloat16)

    @pl.when(g == KV_HEADS - 1)
    def _():
        whole = pltpu.make_async_copy(
            grad.at[pl.ds(0, TOK), :], grad_out.at[pl.ds(0, TOK), :], sems.at[NEED]
        )
        whole.start()

        def give(j, b, i, m, k):
            if m > 0:
                target = mate_out[b][m - 1].at[pl.ds(i * BLK, BLK), :]
            else:
                target = grad_out.at[slot_rows(j), :]
            return pltpu.make_async_copy(grad.at[slot_rows(j), :], target, sems.at[j])

        each_source(GIVE, lambda *at: give(*at).start())
        each_source(GIVE, lambda *at: give(*at).wait())
        whole.wait()


def attend(queries, grads_out, lengths, plan, needed, shards, received):
    block = pl.BlockSpec((TOK, GROUP * HEAD_DIM), lambda g: (0, g))
    ins = [shards[k] for k in COLUMN]
    for arrays in received:
        ins += arrays
    bf = jnp.bfloat16
    outs = [like(TOK, HEADS * HEAD_DIM)] * 2 + [like(KEYS)]
    for offsets in GIVE:
        outs += [like(len(offsets) * BLK)] * 3
    got = pl.pallas_call(
        attend_body,
        grid=(KV_HEADS,),
        out_shape=outs,
        in_specs=[SM] * 3 + [block] * 2 + [ANY] * len(ins),
        out_specs=[block] * 2 + [ANY] * (len(outs) - 2),
        scratch_shapes=[
            pltpu.VMEM((KEYS, 2 * KVW), bf),
            pltpu.VMEM((KEYS, 2 * KVW), bf),
            pltpu.VMEM((KEYS, TOK), jnp.float32),
            pltpu.SMEM((YN * ZN,), jnp.int32),
            pltpu.VMEM((GROUP * TOK, HEAD_DIM), bf),
            pltpu.VMEM((GROUP * TOK, HEAD_DIM), bf),
            pltpu.VMEM((KEYS, GROUP * TOK), bf),
            pltpu.VMEM((KEYS, GROUP * TOK), bf),
            pltpu.SemaphoreType.DMA((NEED + 1,)),
        ],
        compiler_params=pltpu.CompilerParams(vmem_limit_bytes=56 << 20),
        name="attend",
    )(needed, plan, lengths, queries, grads_out, *ins)
    return got[0], got[1], got[2], [got[3 + 3 * b : 6 + 3 * b] for b in range(len(GIVE))]


def combine(needed, grad, arrived, extra, offsets):
    n = len(offsets)
    home = offsets == (0,)

    def body(needed, grad, *refs):
        mates, refs = refs[:3], refs[3:]
        more, refs = refs[: len(extra)], refs[len(extra) :]
        outs, (acc, own, theirs, along, sems) = refs[:-5], refs[-5:]
        z, y = lax.axis_index("z"), lax.axis_index("y")
        me = z * YN + y

        def from_mate(m, i, part):
            src = mates[m - 1].at[pl.ds(i * BLK, BLK), :]
            return pltpu.make_async_copy(src, theirs.at[i, m - 1], sems.at[i, m])

        def own_slots(do):
            for i, k in enumerate(offsets):
                owner = lax.rem(z + k + ZN, ZN) * YN + y
                for j in range(NEED):

                    @pl.when(needed[j, me] // 2 == owner)
                    def _(i=i, j=j):
                        rows = pl.ds(TOK + j * BLK, BLK)
                        do(pltpu.make_async_copy(grad.at[rows, :], own.at[i], sems.at[i, 0]), i, j)

        ring = [
            pltpu.make_async_copy(r, along.at[e], sems.at[n, e]) for e, r in enumerate(more)
        ]
        for c in ring:
            c.start()
        each_listed(needed, offsets, lambda *at: from_mate(*at).start())
        if home:
            mine = pltpu.make_async_copy(grad.at[pl.ds(0, TOK), :], own, sems.at[0, 0])
            mine.start()
            mine.wait()
            acc[0] = own[...].astype(jnp.float32)
        else:
            own_slots(lambda c, i, j: c.start())
            if not ring:
                acc[...] = jnp.zeros_like(acc)
        for e, c in enumerate(ring):
            c.wait()
            if home:
                acc[0] += along[e].astype(jnp.float32)
            else:
                acc[e] = along[e].astype(jnp.float32)
        if n > len(ring) and ring:
            acc[n - 1] = jnp.zeros((TOK, 2 * KVW), jnp.float32)

        def add_mate(m, i, part):
            from_mate(m, i, part).wait()
            half(acc.at[i], part)[...] += theirs[i, m - 1].astype(jnp.float32)

        def add_own(c, i, j):
            c.wait()
            half(acc.at[i], needed[j, me] % 2)[...] += own[i].astype(jnp.float32)

        each_listed(needed, offsets, add_mate)
        if home:
            outs[0][...] = acc[0, :, :KVW].astype(jnp.bfloat16)
            outs[1][...] = acc[0, :, KVW:].astype(jnp.bfloat16)
        else:
            own_slots(add_own)
            for i in range(n):
                outs[i][...] = acc[i].astype(jnp.bfloat16)

    shapes = [like(TOK, KVW)] * 2 if home else [like(TOK)] * n
    return pl.pallas_call(
        body,
        out_shape=shapes,
        in_specs=[SM] + [ANY] * (4 + len(extra)),
        out_specs=[VM] * len(shapes),
        scratch_shapes=[
            pltpu.VMEM((n, TOK, 2 * KVW), jnp.float32),
            pltpu.VMEM((TOK, 2 * KVW) if home else (n, BLK, 2 * KVW), jnp.bfloat16),
            pltpu.VMEM((n, 3, BLK, 2 * KVW), jnp.bfloat16),
            pltpu.VMEM((max(len(extra), 1), TOK, 2 * KVW), jnp.bfloat16),
            pltpu.SemaphoreType.DMA((n + 1, YN)),
        ],
        compiler_params=pltpu.CompilerParams(vmem_limit_bytes=16 << 20),
        name="combine",
    )(needed, grad, *arrived, *extra)


def scatter(grad, mates, needed):
    def hop(arrays):
        return [shift(arrays[0], "z", ZN, 1), shift(arrays[1], "z", ZN, -1)]

    third = to_mates(mates[0], -1)
    second = to_mates(mates[1], -1)
    ring = list(combine(needed, grad, third, [], GIVE[0]))
    first, last, ring[0] = lax.optimization_barrier((mates[2], mates[3], ring[0]))
    first = to_mates(first, -1)
    ring = hop(ring)
    up, down, far = combine(needed, grad, second, ring, GIVE[1])
    last, up = lax.optimization_barrier((last, up))
    far = shift(far, "z", ZN, 4)
    ring = hop([up, down])
    last = to_mates(last, -1)
    ring = hop(combine(needed, grad, first, ring, GIVE[2]))
    return combine(needed, grad, last, ring + [far], GIVE[3])


def on_device(queries, key_states, value_states, grads_out, lengths, plan, needed):
    needed = needed.T
    kv, mine = join(needed, key_states, value_states)
    shards, received = gather(kv, mine, needed)
    outputs, query_grads, grad, mates = attend(
        queries, grads_out, lengths, plan, needed, shards, received
    )
    key_grads, value_grads = scatter(grad, mates, needed)
    return outputs, query_grads, key_grads, value_grads


def solution(mesh):
    torus = Mesh(mesh.devices.reshape(mesh.shape["grp"], ZN, YN), ("grp", "z", "y"))
    rows = P(("grp", "z", "y"), None)
    return jax.shard_map(
        on_device,
        mesh=torus,
        in_specs=(rows, rows, rows, rows, P("grp"), P("grp"), P("grp", None)),
        out_specs=(rows, rows, rows, rows),
        check_vma=False,
    )
```

```python
import math

import jax
import jax.numpy as jnp
from jax import lax
from jax.experimental import pallas as pl
from jax.experimental.pallas import tpu as pltpu
from jax.sharding import Mesh
from jax.sharding import PartitionSpec as P

HEADS = 32
KV_HEADS = 4
HEAD_DIM = 128
GROUP = HEADS // KV_HEADS
BLK = 64
NEED = 8
NDOC = 8
TOK = 128
ZN = 8
YN = 4
KVW = KV_HEADS * HEAD_DIM
KEYS = TOK + NEED * BLK
PAIR = 4 * TOK
SCALE = 1.0 / math.sqrt(HEAD_DIM)
LOG2E = math.log2(math.e)
HIDDEN = -1e30

FETCH = ((0,), (1, -1, 2, -2), (3, -3, 4))
GIVE = ((3, -3), (2, -2, 4), (1, -1), (0,))
COLUMN = (0, 1, -1, 2, -2, 3, -3, 4)

VM = pl.BlockSpec(memory_space=pltpu.VMEM)
ANY = pl.BlockSpec(memory_space=pl.ANY)
SM = pl.BlockSpec(memory_space=pltpu.SMEM)


def half(ref, part):
    return ref.at[pl.ds(pl.multiple_of(part * BLK, BLK), BLK), :]


def like(rows, cols=2 * KVW):
    return jax.ShapeDtypeStruct((rows, cols), jnp.bfloat16)


def listed(needed, rank, block):
    found = jnp.int32(0)
    for j in range(NEED):
        found = jnp.where(needed[j, rank] == block, 1, found)
    return found


def each_listed(needed, offsets, do):
    z, y = lax.axis_index("z"), lax.axis_index("y")
    for i, k in enumerate(offsets):
        owner = lax.rem(z + k + ZN, ZN) * YN + y
        for m in (1, 2, 3):
            rank = z * YN + lax.rem(y + m, YN)
            first, second = (listed(needed, rank, 2 * owner + p) for p in (0, 1))

            @pl.when(first + second > 0)
            def _(i=i, m=m, second=second):
                do(m, i, second)


def pack(needed, shards, offsets):
    count = len(offsets)

    def body(needed, *refs):
        ins, outs, sems = refs[:count], refs[count:-1], refs[-1]

        def copy(m, i, part):
            dst = outs[m - 1].at[pl.ds(i * BLK, BLK), :]
            return pltpu.make_async_copy(half(ins[i], part), dst, sems.at[i, m - 1])

        each_listed(needed, offsets, lambda *at: copy(*at).start())
        each_listed(needed, offsets, lambda *at: copy(*at).wait())

    return pl.pallas_call(
        body,
        out_shape=[like(count * BLK)] * 3,
        in_specs=[SM] + [ANY] * count,
        out_specs=[VM] * 3,
        scratch_shapes=[pltpu.SemaphoreType.DMA((count, 3))],
        name="pack",
    )(needed, *shards)


def shift(array, axis, size, by):
    return lax.ppermute(array, axis, [(i, (i + by) % size) for i in range(size)])


def to_mates(arrays, sign):
    return [shift(a, "y", YN, sign * m) for m, a in zip((1, 2, 3), arrays)]


def join(needed, key_states, value_states):
    def body(needed, k, v, kv, *outs):
        kv[:, :KVW] = k[...]
        kv[:, KVW:] = v[...]

        def copy(m, i, part):
            outs[m - 1][:, :KVW] = half(k, part)[...]
            outs[m - 1][:, KVW:] = half(v, part)[...]

        each_listed(needed, (0,), copy)

    got = pl.pallas_call(
        body,
        out_shape=[like(TOK)] + [like(BLK)] * 3,
        in_specs=[SM, VM, VM],
        out_specs=[VM] * 4,
        name="join",
    )(needed, key_states, value_states)
    return got[0], got[1:]


def gather(kv, mine, needed):
    shards = {0: kv}
    shards[1], shards[-1] = shift(kv, "z", ZN, -1), shift(kv, "z", ZN, 1)
    shards[2], shards[-2] = shift(shards[1], "z", ZN, -1), shift(shards[-1], "z", ZN, 1)
    zeroth = to_mates(mine, 1)

    def packed(b):
        return pack(needed, [shards[k] for k in FETCH[b]], FETCH[b])

    shards[2], zeroth = lax.optimization_barrier((shards[2], zeroth))
    mine = packed(1)
    first = to_mates(mine, 1)
    up, down, mine = lax.optimization_barrier((shards[2], shards[-2], mine))
    shards[3], shards[-3] = shift(up, "z", ZN, -1), shift(down, "z", ZN, 1)
    far, shards[3] = lax.optimization_barrier((kv, shards[3]))
    shards[4] = shift(far, "z", ZN, 4)
    return shards, [zeroth, first, to_mates(packed(2), 1)]


def attend_body(needed, plan, lengths, q_ref, do_ref, *refs):
    shards, refs = dict(zip(COLUMN, refs[:ZN])), refs[ZN:]
    received, refs = [refs[3 * b : 3 * b + 3] for b in range(len(FETCH))], refs[3 * len(FETCH) :]
    o_ref, dq_ref, grad_out, refs = refs[0], refs[1], refs[2], refs[3:]
    mate_out, refs = [refs[3 * b : 3 * b + 3] for b in range(len(GIVE))], refs[3 * len(GIVE) :]
    kv, grad, bias, table, qs, dos, pt, dst, sems = refs
    g = pl.program_id(0)
    z, y = lax.axis_index("z"), lax.axis_index("y")
    me = z * YN + y

    def slot_rows(j):
        return pl.ds(pl.multiple_of(TOK + j * BLK, BLK), BLK)

    def each_source(bundles, do):
        for b, offsets in enumerate(bundles):
            for i, k in enumerate(offsets):
                for m in range(YN):
                    j = table[m * ZN + k % ZN]

                    @pl.when(j >= 0)
                    def _(j=j, b=b, i=i, m=m, k=k):
                        do(j, b, i, m, k)

    @pl.when(g == 0)
    def _():
        own_copy = pltpu.make_async_copy(shards[0], kv.at[pl.ds(0, TOK), :], sems.at[NEED])
        own_copy.start()
        for i in range(YN * ZN):
            table[i] = -1
        for j in range(NEED):
            owner = needed[j, me] // 2
            distance = lax.rem(owner // YN - z + ZN, ZN)
            mate = lax.rem(y - lax.rem(owner, YN) + YN, YN)
            table[mate * ZN + distance] = j

        def fetch(j, b, i, m, k):
            if m == 0:
                src = half(shards[k], needed[j, me] % 2)
            else:
                src = received[b][m - 1].at[pl.ds(i * BLK, BLK), :]
            pltpu.make_async_copy(src, kv.at[slot_rows(j), :], sems.at[j]).start()

        each_source(FETCH, fetch)
        ends, total = [], jnp.int32(0)
        for d in range(NDOC):
            total = total + lengths[d]
            ends.append(total)

        def docs(place):
            found = jnp.zeros_like(place)
            for end in ends:
                found = found + (place >= end).astype(jnp.int32)
            return found

        lane = lax.broadcasted_iota(jnp.int32, (BLK, TOK), 1)
        first = lane < BLK
        q_place = jnp.where(first, plan[2 * me] * BLK, plan[2 * me + 1] * BLK) + lane % BLK
        q_doc = docs(q_place)
        row = lax.broadcasted_iota(jnp.int32, (BLK, TOK), 0)

        def block_bias(block, allowed):
            k_place = plan[block] * BLK + row
            seen = (docs(k_place) == q_doc) & (k_place <= q_place) & allowed
            return jnp.where(seen, 0.0, HIDDEN)

        for half_block in (0, 1):
            block = 2 * me + half_block
            also = listed(needed, me, block)
            same = (lane // BLK) == half_block
            bias[half_block * BLK : (half_block + 1) * BLK, :] = block_bias(
                block, same | ((row * 0 + also) == 1)
            )
        for j in range(NEED):
            block = needed[j, me]
            other = jnp.where(block // 2 == me, 0, 1)
            bias[TOK + j * BLK : TOK + (j + 1) * BLK, :] = block_bias(block, (row * 0 + other) == 1)
        own_copy.wait()
        for j in range(NEED):
            slot = kv.at[pl.ds(TOK + j * BLK, BLK), :]
            pltpu.make_async_copy(half(shards[0], 0), slot, sems.at[j]).wait()

    for h in range(GROUP):
        qs[h * TOK : (h + 1) * TOK, :] = q_ref[:, h * HEAD_DIM : (h + 1) * HEAD_DIM]
        dos[h * TOK : (h + 1) * TOK, :] = do_ref[:, h * HEAD_DIM : (h + 1) * HEAD_DIM]

    k_cols = pl.ds(pl.multiple_of(g * HEAD_DIM, HEAD_DIM), HEAD_DIM)
    v_cols = pl.ds(pl.multiple_of(KVW + g * HEAD_DIM, HEAD_DIM), HEAD_DIM)
    keys, values = kv[:, k_cols], kv[:, v_cols]
    wide_bias = jnp.concatenate([bias[...]] * 4, axis=1)

    def nt(a, b):
        return lax.dot_general(a, b, (((1,), (1,)), ((), ())), preferred_element_type=jnp.float32)

    def tn(a, b):
        return lax.dot_general(a, b, (((0,), (0,)), ((), ())), preferred_element_type=jnp.float32)

    def nn(a, b):
        return jnp.dot(a, b, preferred_element_type=jnp.float32)

    for pair in range(GROUP // 4):
        rows = slice(pair * PAIR, (pair + 1) * PAIR)
        scores = nt(keys, qs[rows, :]) * (SCALE * LOG2E) + wide_bias
        highest = jnp.max(scores, axis=0, keepdims=True)
        weights = jnp.exp2(scores - highest)
        weights = weights * (1.0 / jnp.sum(weights, axis=0, keepdims=True))
        low = weights.astype(jnp.bfloat16)
        pt[:, rows] = low
        prob_grads = nt(values, dos[rows, :])
        delta = jnp.sum(weights * prob_grads, axis=0, keepdims=True)
        score_grads = (weights * (prob_grads - delta)).astype(jnp.bfloat16)
        dst[:, rows] = score_grads
    out = tn(pt[...], values)
    dq = tn(dst[...], keys) * SCALE
    for h in range(GROUP):
        cols, rows = slice(h * HEAD_DIM, (h + 1) * HEAD_DIM), slice(h * TOK, (h + 1) * TOK)
        o_ref[:, cols] = out[rows, :].astype(jnp.bfloat16)
        dq_ref[:, cols] = dq[rows, :].astype(jnp.bfloat16)
    grad[:, k_cols] = (nn(dst[...], qs[...]) * SCALE).astype(jnp.bfloat16)
    grad[:, v_cols] = nn(pt[...], dos[...]).astype(jnp.bfloat16)

    @pl.when(g == KV_HEADS - 1)
    def _():
        whole = pltpu.make_async_copy(
            grad.at[pl.ds(0, TOK), :], grad_out.at[pl.ds(0, TOK), :], sems.at[NEED]
        )
        whole.start()

        def give(j, b, i, m, k):
            if m > 0:
                target = mate_out[b][m - 1].at[pl.ds(i * BLK, BLK), :]
            else:
                target = grad_out.at[slot_rows(j), :]
            return pltpu.make_async_copy(grad.at[slot_rows(j), :], target, sems.at[j])

        each_source(GIVE, lambda *at: give(*at).start())
        each_source(GIVE, lambda *at: give(*at).wait())
        whole.wait()


def attend(queries, grads_out, lengths, plan, needed, shards, received):
    block = pl.BlockSpec((TOK, GROUP * HEAD_DIM), lambda g: (0, g))
    ins = [shards[k] for k in COLUMN]
    for arrays in received:
        ins += arrays
    bf = jnp.bfloat16
    outs = [like(TOK, HEADS * HEAD_DIM)] * 2 + [like(KEYS)]
    for offsets in GIVE:
        outs += [like(len(offsets) * BLK)] * 3
    got = pl.pallas_call(
        attend_body,
        grid=(KV_HEADS,),
        out_shape=outs,
        in_specs=[SM] * 3 + [block] * 2 + [ANY] * len(ins),
        out_specs=[block] * 2 + [ANY] * (len(outs) - 2),
        scratch_shapes=[
            pltpu.VMEM((KEYS, 2 * KVW), bf),
            pltpu.VMEM((KEYS, 2 * KVW), bf),
            pltpu.VMEM((KEYS, TOK), jnp.float32),
            pltpu.SMEM((YN * ZN,), jnp.int32),
            pltpu.VMEM((GROUP * TOK, HEAD_DIM), bf),
            pltpu.VMEM((GROUP * TOK, HEAD_DIM), bf),
            pltpu.VMEM((KEYS, GROUP * TOK), bf),
            pltpu.VMEM((KEYS, GROUP * TOK), bf),
            pltpu.SemaphoreType.DMA((NEED + 1,)),
        ],
        compiler_params=pltpu.CompilerParams(vmem_limit_bytes=56 << 20),
        name="attend",
    )(needed, plan, lengths, queries, grads_out, *ins)
    return got[0], got[1], got[2], [got[3 + 3 * b : 6 + 3 * b] for b in range(len(GIVE))]


def combine(needed, grad, arrived, extra, offsets):
    n = len(offsets)
    home = offsets == (0,)

    def body(needed, grad, *refs):
        mates, refs = refs[:3], refs[3:]
        more, refs = refs[: len(extra)], refs[len(extra) :]
        outs, (acc, own, theirs, along, sems) = refs[:-5], refs[-5:]
        z, y = lax.axis_index("z"), lax.axis_index("y")
        me = z * YN + y

        def from_mate(m, i, part):
            src = mates[m - 1].at[pl.ds(i * BLK, BLK), :]
            return pltpu.make_async_copy(src, theirs.at[i, m - 1], sems.at[i, m])

        def own_slots(do):
            for i, k in enumerate(offsets):
                owner = lax.rem(z + k + ZN, ZN) * YN + y
                for j in range(NEED):

                    @pl.when(needed[j, me] // 2 == owner)
                    def _(i=i, j=j):
                        rows = pl.ds(TOK + j * BLK, BLK)
                        do(pltpu.make_async_copy(grad.at[rows, :], own.at[i], sems.at[i, 0]), i, j)

        ring = [
            pltpu.make_async_copy(r, along.at[e], sems.at[n, e]) for e, r in enumerate(more)
        ]
        for c in ring:
            c.start()
        each_listed(needed, offsets, lambda *at: from_mate(*at).start())
        if home:
            mine = pltpu.make_async_copy(grad.at[pl.ds(0, TOK), :], own, sems.at[0, 0])
            mine.start()
            mine.wait()
            acc[0] = own[...].astype(jnp.float32)
        else:
            own_slots(lambda c, i, j: c.start())
            if not ring:
                acc[...] = jnp.zeros_like(acc)
        for e, c in enumerate(ring):
            c.wait()
            if home:
                acc[0] += along[e].astype(jnp.float32)
            else:
                acc[e] = along[e].astype(jnp.float32)
        if n > len(ring) and ring:
            acc[n - 1] = jnp.zeros((TOK, 2 * KVW), jnp.float32)

        def add_mate(m, i, part):
            from_mate(m, i, part).wait()
            half(acc.at[i], part)[...] += theirs[i, m - 1].astype(jnp.float32)

        def add_own(c, i, j):
            c.wait()
            half(acc.at[i], needed[j, me] % 2)[...] += own[i].astype(jnp.float32)

        each_listed(needed, offsets, add_mate)
        if home:
            outs[0][...] = acc[0, :, :KVW].astype(jnp.bfloat16)
            outs[1][...] = acc[0, :, KVW:].astype(jnp.bfloat16)
        else:
            own_slots(add_own)
            for i in range(n):
                outs[i][...] = acc[i].astype(jnp.bfloat16)

    shapes = [like(TOK, KVW)] * 2 if home else [like(TOK)] * n
    return pl.pallas_call(
        body,
        out_shape=shapes,
        in_specs=[SM] + [ANY] * (4 + len(extra)),
        out_specs=[VM] * len(shapes),
        scratch_shapes=[
            pltpu.VMEM((n, TOK, 2 * KVW), jnp.float32),
            pltpu.VMEM((TOK, 2 * KVW) if home else (n, BLK, 2 * KVW), jnp.bfloat16),
            pltpu.VMEM((n, 3, BLK, 2 * KVW), jnp.bfloat16),
            pltpu.VMEM((max(len(extra), 1), TOK, 2 * KVW), jnp.bfloat16),
            pltpu.SemaphoreType.DMA((n + 1, YN)),
        ],
        compiler_params=pltpu.CompilerParams(vmem_limit_bytes=16 << 20),
        name="combine",
    )(needed, grad, *arrived, *extra)


def scatter(grad, mates, needed):
    def hop(arrays):
        return [shift(arrays[0], "z", ZN, 1), shift(arrays[1], "z", ZN, -1)]

    third = to_mates(mates[0], -1)
    second = to_mates(mates[1], -1)
    ring = list(combine(needed, grad, third, [], GIVE[0]))
    first, last, ring[0] = lax.optimization_barrier((mates[2], mates[3], ring[0]))
    first = to_mates(first, -1)
    ring = hop(ring)
    up, down, far = combine(needed, grad, second, ring, GIVE[1])
    last, up = lax.optimization_barrier((last, up))
    far = shift(far, "z", ZN, 4)
    ring = hop([up, down])
    last = to_mates(last, -1)
    ring = hop(combine(needed, grad, first, ring, GIVE[2]))
    return combine(needed, grad, last, ring + [far], GIVE[3])


def on_device(queries, key_states, value_states, grads_out, lengths, plan, needed):
    needed = needed.T
    kv, mine = join(needed, key_states, value_states)
    shards, received = gather(kv, mine, needed)
    outputs, query_grads, grad, mates = attend(
        queries, grads_out, lengths, plan, needed, shards, received
    )
    key_grads, value_grads = scatter(grad, mates, needed)
    return outputs, query_grads, key_grads, value_grads


def solution(mesh):
    torus = Mesh(mesh.devices.reshape(mesh.shape["grp"], ZN, YN), ("grp", "z", "y"))
    rows = P(("grp", "z", "y"), None)
    return jax.shard_map(
        on_device,
        mesh=torus,
        in_specs=(rows, rows, rows, rows, P("grp"), P("grp"), P("grp", None)),
        out_specs=(rows, rows, rows, rows),
        check_vma=False,
    )
```
